32 devices in a mesh: people: 8 (over z, x), snps: 4 (over y, core).
Axes of the slice: x: 2, y: 2, z: 4, core: 2. Of those that a mesh axis runs over, the one named last changes fastest.
Arguments:
- genotype: bfloat16 [4096, 16384], P('people', 'snps'), may hold values from 0 to 2, as said below
- residual_init: float32 [32, 4096], P(None, 'people'), may hold values from -30 to 30
- effects_init: float32 [32, 16384], P(None, 'snps'), may hold values from -3 to 3
- allele_freq: float32 [16384], P('snps'), may hold values from 0.05 to 0.5, as said below
- snp_scale: float32 [16384], P('snps'), may hold values from 0.8 to 1.25
- ld_basis: bfloat16 [32, 512, 512], P('snps'), may hold values from -1 to 1, as said below
- ld_eig: float32 [16384], P('snps'), may hold values from 0.5 to 2
- ridge: float32 [32], replicated, may hold values from 1.5 to 4
- noise_scale: float32 [32], replicated, may hold values from 0.2 to 1
- normal_draws: bfloat16 [4, 32, 16384], P(None, None, 'snps'), may hold values from -5 to 5
- assignment: int32 [32], P('snps'), may hold values from 0 to 7, as said below
Outputs:
- effects: float32 [32, 16384], P(None, 'snps')
- residual: float32 [32, 4096], P(None, 'people')
The draws below stay inside these ranges and needn't reach their ends.
Inputs may be any that keep to these rules, and one draw needn't show every extreme that they name: `assignment`: the 8 entries that lie on one index of snps are each a permutation of 0 to 7. `ld_basis`: each block's basis is orthogonal up to its rounding to bfloat16. `genotype`: only the values 0, 1 and 2 occur; each dosage counts two alleles, each present with the SNP's allele_freq. `allele_freq`: multiples of 0.001.
All inputs are finite; a program needn't handle non-finite values.
Results may differ from the reference program's by a relative error of at most 0.014.
Values sent between devices are 32-bit elements; how exact they have to be, the bound alone decides.
A program may use at most 64 MiB of HBM per device.

```python
import math
import jax
import jax.numpy as jnp
from jax import lax

K = 32
BS = 512
WINDOW = 4
GROUPS_DEV = 2
ROUNDS = 4
PEOPLE = 4096
BLOCKS_DEV = 8
NBLOCKS = 32
GROUPS = 8
SNPS = 16384


def freq_units(key):
    return jax.random.randint(jax.random.fold_in(key, 7), (SNPS,), 50, 501)


def draw_allele_freq(key, part):
    return freq_units(key).astype(jnp.float32) / 1000.0


def draw_genotype(key, part):
    units = freq_units(key)
    first_key = jax.random.fold_in(key, 11)
    second_key = jax.random.fold_in(key, 13)
    first_allele = (jax.random.randint(first_key, (PEOPLE, SNPS), 0, 1000) < units[None, :]).astype(jnp.int32)
    second_allele = (jax.random.randint(second_key, (PEOPLE, SNPS), 0, 1000) < units[None, :]).astype(jnp.int32)
    dosage = first_allele + second_allele
    return dosage.astype(jnp.float32).astype(jnp.bfloat16)


def draw_residual_init(key, part):
    first_key, second_key = jax.random.split(key, 2)
    position = jnp.arange(PEOPLE, dtype=jnp.float32) / PEOPLE
    level = jnp.exp(jnp.log(10.0) * jax.random.uniform(second_key, (PEOPLE,), jnp.float32))
    row_scale = 0.25 * level * (1.0 + 2.0 * position)
    base = jnp.clip(jax.random.normal(first_key, (K, PEOPLE), jnp.float32), -4.0, 4.0)
    return base * row_scale[None, :]


def orthogonal_block(single_key):
    gaussian = jax.random.normal(single_key, (BS, BS), jnp.float32)
    basis, upper = jnp.linalg.qr(gaussian)
    return basis


def draw_ld_basis(key, part):
    block_keys = jax.random.split(key, NBLOCKS)
    bases = lax.map(orthogonal_block, block_keys)
    return jnp.clip(bases, -1.0, 1.0).astype(jnp.bfloat16)


def draw_assignment(key, part):
    device_keys = jax.random.split(key, NBLOCKS // BLOCKS_DEV)
    orders = jax.vmap(lambda single: jax.random.permutation(single, BLOCKS_DEV))(device_keys)
    return orders.reshape(-1).astype(jnp.int32)


def block_levels(stream_key, dims, pieces, smallest, top_value):
    def one(dim, parts):
        steps = jax.random.uniform(jax.random.fold_in(jax.random.fold_in(stream_key, 6), dim), (parts,), jnp.float32, smallest / len(pieces), top_value / len(pieces))
        return jnp.repeat(jnp.exp(steps), dims[dim] // parts).reshape((-1,) + (1,) * (len(dims) - dim - 1))

    loudness = one(*pieces[0])
    for cut in pieces[1:]:
        loudness = loudness * one(*cut)
    return loudness


def bell_draw(key, dims, width, reach, shards=(), held_as=jnp.bfloat16):
    drawn = width * jax.random.normal(key, dims, jnp.float32)
    if shards:
        drawn = drawn * block_levels(key, dims, shards, -0.22, 0.18)
    return jnp.clip(drawn, -reach, reach).astype(held_as)


def setup_inputs(seed: int = 0) -> dict:
    streams_of = jax.random.split(jax.random.key(seed), 12)
    return {
        "genotype": draw_genotype(jax.random.fold_in(streams_of[11], 71), 0),
        "residual_init": draw_residual_init(jax.random.fold_in(streams_of[11], 71), 0),
        "effects_init": bell_draw(streams_of[2], (K, SNPS), 0.5, 3.0, ((1, 4),), jnp.float32),
        "allele_freq": draw_allele_freq(jax.random.fold_in(streams_of[11], 71), 0),
        "snp_scale": jnp.clip(jnp.exp(math.log(1.25) - 0.4462871 * jax.random.uniform(streams_of[4], (SNPS,), jnp.float32) ** block_levels(streams_of[4], (SNPS,), ((0, 4),), -0.2, 0.2)), 0.8, 1.25),
        "ld_basis": draw_ld_basis(jax.random.fold_in(streams_of[11], 71), 0),
        "ld_eig": jnp.clip(jnp.exp(math.log(2.0) - 1.3862944 * jax.random.uniform(streams_of[6], (SNPS,), jnp.float32) ** block_levels(streams_of[6], (SNPS,), ((0, 4),), -0.2, 0.2)), 0.5, 2.0),
        "ridge": jnp.clip(jnp.exp(jax.random.uniform(streams_of[7], (K,), jnp.float32, math.log(1.5), math.log(4.0))), 1.5, 4.0),
        "noise_scale": jnp.clip(jnp.exp(jax.random.uniform(streams_of[8], (K,), jnp.float32, math.log(0.2), math.log(1.0))), 0.2, 1.0),
        "normal_draws": bell_draw(streams_of[9], (ROUNDS, K, SNPS), 1.0, 5.0, ((2, 4),)),
        "assignment": draw_assignment(jax.random.fold_in(streams_of[11], 71), 0),
    }


def narrow(values):
    return lax.optimization_barrier(values.astype(jnp.bfloat16)).astype(jnp.float32)

def matmul(left, right):
    return jnp.dot(left.astype(jnp.float32), right.astype(jnp.float32), precision=lax.Precision.HIGHEST, preferred_element_type=jnp.float32)

def reference(genotype, residual_init, effects_init, allele_freq, snp_scale, ld_basis, ld_eig, ridge, noise_scale, normal_draws, assignment):
    col_scale = snp_scale / jnp.sqrt(PEOPLE * 2.0 * allele_freq * (1.0 - allele_freq))
    residual = residual_init
    effects = effects_init
    for round_idx in range(ROUNDS):
        spread = noise_scale * jnp.sqrt(lax.optimization_barrier(jnp.sum(residual * residual, axis=1)) / PEOPLE + 1e-06)
        changes = jnp.zeros_like(residual)
        for group_idx in range(GROUPS):
            device_idx = group_idx // GROUPS_DEV
            member = group_idx % GROUPS_DEV
            state = residual
            for slot_idx in range(WINDOW):
                local_block = assignment[device_idx * BLOCKS_DEV + member * WINDOW + slot_idx]
                block_idx = (device_idx * BLOCKS_DEV + local_block).astype(jnp.int32)
                col_start = (block_idx * BS).astype(jnp.int32)
                block_x = lax.dynamic_slice_in_dim(genotype, col_start, BS, 1).astype(jnp.float32)
                block_basis = lax.dynamic_index_in_dim(ld_basis, block_idx, 0, keepdims=False).astype(jnp.float32)
                block_eig = lax.dynamic_slice_in_dim(ld_eig, col_start, BS, 0)
                block_freq = lax.dynamic_slice_in_dim(allele_freq, col_start, BS, 0)
                block_scale = lax.dynamic_slice_in_dim(col_scale, col_start, BS, 0)
                old_effects = lax.dynamic_slice_in_dim(effects, col_start, BS, 1)
                draws_block = lax.dynamic_slice_in_dim(normal_draws[round_idx], col_start, BS, 1).astype(jnp.float32)
                cross_term = matmul(narrow(state), block_x)
                data = block_scale[None, :] * (cross_term - 2.0 * block_freq[None, :] * lax.optimization_barrier(jnp.sum(state, axis=1))[:, None])
                prior = matmul(narrow(old_effects), block_basis)
                coupled = matmul(narrow(prior * block_eig[None, :]), block_basis.T)
                rotated = matmul(narrow(data + coupled), block_basis)
                precision = block_eig[None, :] + ridge[:, None]
                sampled = narrow(rotated / precision + spread[:, None] * draws_block / jnp.sqrt(precision))
                fresh = matmul(sampled, block_basis.T)
                change = fresh - old_effects
                effects = lax.dynamic_update_slice_in_dim(effects, fresh, col_start, 1)
                weighted = change * block_scale[None, :]
                shift_term = 2.0 * lax.optimization_barrier(jnp.sum(weighted * block_freq[None, :], axis=1))
                state = state - matmul(narrow(weighted), block_x.T) + shift_term[:, None]
            changes = changes + (state - residual)
        residual = residual + changes
    return (effects, residual)
```

```python
import functools

import jax
import jax.numpy as jnp
from jax import lax
from jax.experimental import pallas as pl
from jax.experimental.pallas import tpu as pltpu
from jax.sharding import PartitionSpec as P

WINDOW = 4
GROUPS_DEV = 2
VMEM = pltpu.MemorySpace.VMEM
LIMIT = 56 * 1024 * 1024


def dot(left, right):
    return jnp.dot(left, right, preferred_element_type=jnp.float32)


def dot_t(left, right):
    return lax.dot_general(
        left, right, (((1,), (1,)), ((), ())), preferred_element_type=jnp.float32
    )


def permute_kernel(
    people_total, order, x, basis, effects, draws, freq, scale, eig,
    x_out, basis_out, effects_out, draws_out, freq_out, scale_out, eig_out,
):
    x_out[0] = x[...]
    basis_out[...] = basis[...]
    effects_out[0] = effects[...]
    draws_out[:, 0] = draws[...].astype(jnp.float32)
    allele = freq[...]
    freq_out[...] = allele
    scale_out[...] = scale[...] / jnp.sqrt(people_total * 2.0 * allele * (1.0 - allele))
    eig_out[...] = eig[...]


def to_slots(people_total, assignment, genotype, ld_basis, effects, draws, freq, scale, eig):
    blocks, width = ld_basis.shape[0], ld_basis.shape[1]
    people = genotype.shape[0]
    traits = effects.shape[0]
    rounds = draws.shape[0]
    row = lambda s, a: (a[s], 0, 0)
    row_out = lambda s, a: (s, 0, 0)
    return pl.pallas_call(
        functools.partial(permute_kernel, people_total),
        grid_spec=pltpu.PrefetchScalarGridSpec(
            num_scalar_prefetch=1,
            grid=(blocks,),
            in_specs=[
                pl.BlockSpec((people, width), lambda s, a: (0, a[s])),
                pl.BlockSpec((1, width, width), row),
                pl.BlockSpec((traits, width), lambda s, a: (0, a[s])),
                pl.BlockSpec((rounds, traits, width), lambda s, a: (0, 0, a[s])),
                pl.BlockSpec((1, 1, width), row),
                pl.BlockSpec((1, 1, width), row),
                pl.BlockSpec((1, 1, width), row),
            ],
            out_specs=[
                pl.BlockSpec((1, people, width), row_out),
                pl.BlockSpec((1, width, width), row_out),
                pl.BlockSpec((1, traits, width), row_out),
                pl.BlockSpec((rounds, 1, traits, width), lambda s, a: (0, s, 0, 0)),
                pl.BlockSpec((1, 1, width), row_out),
                pl.BlockSpec((1, 1, width), row_out),
                pl.BlockSpec((1, 1, width), row_out),
            ],
        ),
        out_shape=[
            jax.ShapeDtypeStruct((blocks, people, width), genotype.dtype),
            jax.ShapeDtypeStruct((blocks, width, width), ld_basis.dtype),
            jax.ShapeDtypeStruct((blocks, traits, width), jnp.float32),
            jax.ShapeDtypeStruct((rounds, blocks, traits, width), jnp.float32),
            jax.ShapeDtypeStruct((blocks, 1, width), jnp.float32),
            jax.ShapeDtypeStruct((blocks, 1, width), jnp.float32),
            jax.ShapeDtypeStruct((blocks, 1, width), jnp.float32),
        ],
        name="to_slots",
    )(
        assignment, genotype, ld_basis, effects, draws,
        freq.reshape(blocks, 1, width), scale.reshape(blocks, 1, width),
        eig.reshape(blocks, 1, width),
    )


def unpermute_kernel(order, source, target):
    target[...] = source[0]


def from_slots(assignment, effects):
    blocks, traits, width = effects.shape
    return pl.pallas_call(
        unpermute_kernel,
        grid_spec=pltpu.PrefetchScalarGridSpec(
            num_scalar_prefetch=1,
            grid=(blocks,),
            in_specs=[pl.BlockSpec((1, traits, width), lambda s, a: (s, 0, 0))],
            out_specs=pl.BlockSpec((traits, width), lambda s, a: (0, a[s])),
        ),
        out_shape=jax.ShapeDtypeStruct((traits, blocks * width), jnp.float32),
        name="from_slots",
    )(assignment, effects)


def gibbs_kernel(
    people_n, snps_n, people_total,
    x, basis, effects_in, draws, freq, scale, eig, ridge, noise, residual_in,
    effects, residual,
    states, part, gathered, changes, deltas, own_effects,
    part_send, part_recv, change_send, change_recv, delta_send, delta_recv,
):
    me = lax.axis_index("people")
    my_snps = lax.axis_index("snps")
    traits, people = residual_in.shape
    width = scale.shape[-1]
    rounds = draws.shape[0]
    rows = GROUPS_DEV * traits // people_n
    subs = traits // rows
    my_group = me // subs
    my_sub = me % subs

    barrier = pltpu.get_barrier_semaphore()
    for step in range(1, people_n):
        pl.semaphore_signal(
            barrier, inc=1, device_id={"people": lax.rem(me + step, people_n)},
            device_id_type=pl.DeviceIdType.MESH,
        )
    for step in range(1, snps_n):
        pl.semaphore_signal(
            barrier, inc=1, device_id={"snps": lax.rem(my_snps + step, snps_n)},
            device_id_type=pl.DeviceIdType.MESH,
        )

    residual[...] = residual_in[...]
    effects[...] = effects_in[...]
    for group in range(GROUPS_DEV):
        states[group] = residual_in[...]
    mine = pl.ds(my_sub * rows, rows)
    for slot in range(WINDOW):
        own_effects[slot] = effects_in[my_group * WINDOW + slot, mine, :]
    my_ridge = ridge[mine, :]
    my_noise = noise[mine, :]
    pl.semaphore_wait(barrier, people_n - 1 + snps_n - 1)

    def round_body(round_idx, carry):
        squares = jnp.sum(residual[...] * residual[...], axis=1, keepdims=True)
        spread = None
        for slot in range(WINDOW):
            for group in range(GROUPS_DEV):
                block = group * WINDOW + slot
                state = states[group]
                cross = dot(state.astype(jnp.bfloat16), x[block])
                cross = cross - 2.0 * freq[block] * jnp.sum(state, axis=1, keepdims=True)
                for sub in range(subs):
                    part[group * subs + sub, :, :width] = cross[sub * rows:(sub + 1) * rows]
                    if slot == 0:
                        part[group * subs + sub, :, width:] = jnp.broadcast_to(
                            squares[sub * rows:(sub + 1) * rows], (rows, 128)
                        )
            span = width + 128 if slot == 0 else width
            part_copies = []
            for step in range(1, people_n):
                target = lax.rem(me + step, people_n)
                copy = pltpu.make_async_remote_copy(
                    src_ref=part.at[target, :, pl.ds(0, span)],
                    dst_ref=gathered.at[step, :, pl.ds(0, span)],
                    send_sem=part_send.at[step],
                    recv_sem=part_recv.at[step],
                    device_id={"people": target},
                    device_id_type=pl.DeviceIdType.MESH,
                )
                copy.start()
                part_copies.append(copy)

            my_block = my_group * WINDOW + slot
            my_basis = basis[my_block]
            my_eig = eig[my_block]
            my_scale = scale[my_block]
            old = own_effects[slot]
            prior = dot(old.astype(jnp.bfloat16), my_basis)
            coupled = dot_t((prior * my_eig).astype(jnp.bfloat16), my_basis)
            precision = my_eig + my_ridge
            jitter = draws[round_idx, my_block, mine, :] / jnp.sqrt(precision)

            for copy in part_copies:
                copy.wait_recv()
            total = part[me, :, :width]
            for step in range(1, people_n):
                total = total + gathered[step, :, :width]
            if slot == 0:
                total_squares = part[me, :, width:]
                for step in range(1, people_n):
                    total_squares = total_squares + gathered[step, :, width:]
                spread = my_noise * jnp.sqrt(total_squares[:, :1] / people_total + 1e-06)
            rotated = dot((my_scale * total + coupled).astype(jnp.bfloat16), my_basis)
            sampled = rotated / precision + spread * jitter
            fresh = dot_t(sampled.astype(jnp.bfloat16), my_basis)
            own_effects[slot] = fresh
            changes[me] = fresh - old

            change_copies = []
            for step in range(1, people_n):
                target = lax.rem(me + step, people_n)
                copy = pltpu.make_async_remote_copy(
                    src_ref=changes.at[me],
                    dst_ref=changes.at[me],
                    send_sem=change_send.at[step],
                    recv_sem=change_recv.at[step],
                    device_id={"people": target},
                    device_id_type=pl.DeviceIdType.MESH,
                )
                copy.start()
                change_copies.append(copy)
            for copy in part_copies:
                copy.wait_send()
            for copy in change_copies:
                copy.wait()
            for group in range(GROUPS_DEV):
                block = group * WINDOW + slot
                pieces = [changes[group * subs + sub] for sub in range(subs)]
                change = pieces[0] if subs == 1 else jnp.concatenate(pieces, axis=0)
                weighted = change * scale[block]
                shift = 2.0 * jnp.sum(weighted * freq[block], axis=1, keepdims=True)
                states[group] = (
                    states[group] - dot_t(weighted.astype(jnp.bfloat16), x[block]) + shift
                )
                effects[block] = effects[block] + change

        bank = lax.rem(round_idx, 2)
        delta = states[0] - residual[...]
        for group in range(1, GROUPS_DEV):
            delta = delta + (states[group] - residual[...])
        deltas[bank, my_snps] = delta
        delta_copies = []
        for step in range(1, snps_n):
            target = lax.rem(my_snps + step, snps_n)
            copy = pltpu.make_async_remote_copy(
                src_ref=deltas.at[bank, my_snps],
                dst_ref=deltas.at[bank, my_snps],
                send_sem=delta_send.at[bank, step],
                recv_sem=delta_recv.at[bank, step],
                device_id={"snps": target},
                device_id_type=pl.DeviceIdType.MESH,
            )
            copy.start()
            delta_copies.append(copy)
        for copy in delta_copies:
            copy.wait()
        total = deltas[bank, 0]
        for index in range(1, snps_n):
            total = total + deltas[bank, index]
        fresh_residual = residual[...] + total
        residual[...] = fresh_residual
        for group in range(GROUPS_DEV):
            states[group] = fresh_residual
        return carry

    lax.fori_loop(0, rounds, round_body, 0)


def per_device(people_n, snps_n, genotype, residual_init, effects_init, allele_freq, snp_scale,
               ld_basis, ld_eig, ridge, noise_scale, normal_draws, assignment):
    traits, people = residual_init.shape
    width = ld_basis.shape[1]
    people_total = people * people_n
    x, basis, effects_in, draws, freq, scale, eig = to_slots(
        people_total, assignment, genotype, ld_basis, effects_init, normal_draws,
        allele_freq, snp_scale, ld_eig,
    )
    rows = GROUPS_DEV * traits // people_n
    effects, residual = pl.pallas_call(
        functools.partial(gibbs_kernel, people_n, snps_n, people_total),
        out_shape=[
            jax.ShapeDtypeStruct(effects_in.shape, jnp.float32),
            jax.ShapeDtypeStruct((traits, people), jnp.float32),
        ],
        in_specs=[pl.BlockSpec(memory_space=VMEM)] * 10,
        out_specs=[pl.BlockSpec(memory_space=VMEM)] * 2,
        scratch_shapes=[
            pltpu.VMEM((GROUPS_DEV, traits, people), jnp.float32),
            pltpu.VMEM((people_n, rows, width + 128), jnp.float32),
            pltpu.VMEM((people_n, rows, width + 128), jnp.float32),
            pltpu.VMEM((people_n, rows, width), jnp.float32),
            pltpu.VMEM((2, snps_n, traits, people), jnp.float32),
            pltpu.VMEM((WINDOW, rows, width), jnp.float32),
            pltpu.SemaphoreType.DMA((people_n,)),
            pltpu.SemaphoreType.DMA((people_n,)),
            pltpu.SemaphoreType.DMA((people_n,)),
            pltpu.SemaphoreType.DMA((people_n,)),
            pltpu.SemaphoreType.DMA((2, snps_n)),
            pltpu.SemaphoreType.DMA((2, snps_n)),
        ],
        compiler_params=pltpu.CompilerParams(
            collective_id=0, has_side_effects=True, vmem_limit_bytes=LIMIT
        ),
        name="gibbs",
    )(
        x, basis, effects_in, draws, freq, scale, eig,
        ridge.reshape(traits, 1), noise_scale.reshape(traits, 1), residual_init,
    )
    return from_slots(assignment, effects), residual


def solution(mesh):
    return jax.shard_map(
        functools.partial(per_device, mesh.shape["people"], mesh.shape["snps"]),
        mesh=mesh,
        in_specs=(
            P("people", "snps"),
            P(None, "people"),
            P(None, "snps"),
            P("snps"),
            P("snps"),
            P("snps", None, None),
            P("snps"),
            P(),
            P(),
            P(None, None, "snps"),
            P("snps"),
        ),
        out_specs=(P(None, "snps"), P(None, "people")),
        check_vma=False,
    )
```

```python
import functools

import jax
import jax.numpy as jnp
from jax import lax
from jax.experimental import pallas as pl
from jax.experimental.pallas import tpu as pltpu
from jax.sharding import PartitionSpec as P

WINDOW = 4
GROUPS_DEV = 2
LIMIT = 56 * 1024 * 1024
MESH = pl.DeviceIdType.MESH


def dot(left, right):
    return jnp.dot(left, right, preferred_element_type=jnp.float32)


def dot_t(left, right):
    return lax.dot_general(
        left, right, (((1,), (1,)), ((), ())), preferred_element_type=jnp.float32
    )


def as_column(row):
    size = row.shape[1]
    across = lax.broadcasted_iota(jnp.int32, (size, size), 1)
    down = lax.broadcasted_iota(jnp.int32, (size, size), 0)
    spread_out = jnp.broadcast_to(row, (size, size))
    return jnp.sum(jnp.where(across == down, spread_out, 0.0), axis=1, keepdims=True)


def gibbs_kernel(
    people_n, snps_n, people_total,
    genotype_hbm, basis_hbm, draws_hbm, effects_hbm, freq, snp_scale, eig, ridge, noise,
    residual_in, assignment, inverse,
    effects, residual,
    genotype, basis, draws, effects_in, scale, slot_effects, states, part, gathered, changes, deltas,
    own_effects, own_draws, own_traits, own_spread,
    load_sem, part_send, part_recv, change_send, change_recv, delta_send, delta_recv,
):
    me = lax.axis_index("people")
    my_snps = lax.axis_index("snps")
    traits, people = residual_in.shape
    blocks, width = basis.shape[0], basis.shape[1]
    rounds = draws.shape[1]
    owners, rows = part.shape[0], part.shape[1]
    first = (people_n - owners) // 2
    subs = owners // GROUPS_DEV
    owner_here = (me >= first) & (me < first + owners)
    mine = me - first
    my_group = mine // subs
    my_rows = pl.ds((mine % subs) * rows, rows)

    loads = [pltpu.make_async_copy(basis_hbm, basis, load_sem.at[3 * blocks])]
    for block in range(blocks):
        cols = pl.ds(block * width, width)
        loads += [
            pltpu.make_async_copy(effects_hbm.at[:, cols], effects_in.at[block], load_sem.at[block]),
            pltpu.make_async_copy(
                genotype_hbm.at[:, cols], genotype.at[block], load_sem.at[blocks + block]
            ),
            pltpu.make_async_copy(
                draws_hbm.at[:, :, cols], draws.at[block], load_sem.at[2 * blocks + block]
            ),
        ]
    for load in loads:
        load.start()

    barrier = pltpu.get_barrier_semaphore()
    for step in range(1, people_n):
        pl.semaphore_signal(
            barrier, inc=1, device_id={"people": lax.rem(me + step, people_n)},
            device_id_type=MESH,
        )
    for step in range(1, snps_n):
        pl.semaphore_signal(
            barrier, inc=1, device_id={"snps": lax.rem(my_snps + step, snps_n)},
            device_id_type=MESH,
        )

    allele = freq[...]
    scale[...] = snp_scale[...] / jnp.sqrt(people_total * 2.0 * allele * (1.0 - allele))
    residual[...] = residual_in[...]
    for group in range(GROUPS_DEV):
        states[group] = residual_in[...]
    own_traits[0] = jnp.broadcast_to(as_column(ridge[...]), (traits, 128))
    own_traits[1] = jnp.broadcast_to(as_column(noise[...]), (traits, 128))

    def part_copy(owner, step, span):
        return pltpu.make_async_remote_copy(
            src_ref=part.at[owner - first, :, pl.ds(0, span)],
            dst_ref=gathered.at[step, :, pl.ds(0, span)],
            send_sem=part_send.at[owner - first],
            recv_sem=part_recv.at[step],
            device_id={"people": owner},
            device_id_type=MESH,
        )

    def change_copy(owner, target, bank):
        return pltpu.make_async_remote_copy(
            src_ref=changes.at[bank, owner],
            dst_ref=changes.at[bank, owner],
            send_sem=change_send.at[bank, target],
            recv_sem=change_recv.at[bank, owner],
            device_id={"people": target},
            device_id_type=MESH,
        )

    def far_first(index, count):
        return jnp.where(me < people_n // 2, count - 1 - index, index)

    def span_of(slot):
        return width + 128 if slot == 0 else width

    def send_parts(slot, group, squares):
        block = group * WINDOW + slot
        held = assignment[block]
        state = states[group]
        cross = dot(state.astype(jnp.bfloat16), genotype[held])
        cross = cross - 2.0 * freq[held] * jnp.sum(state, axis=1, keepdims=True)
        for sub in range(subs):
            owner = group * subs + sub
            part[owner, :, :width] = cross[sub * rows:(sub + 1) * rows]
            if slot == 0:
                part[owner, :, width:] = jnp.broadcast_to(
                    squares[sub * rows:(sub + 1) * rows], (rows, 128)
                )
        for index in range(subs):
            owner = first + group * subs + far_first(index, subs)

            @pl.when(owner != me)
            def _():
                part_copy(owner, lax.rem(me - owner + people_n, people_n), span_of(slot)).start()

    def sample(round_idx, slot):
        bank = slot % 2
        my_block = my_group * WINDOW + slot
        held = assignment[my_block]
        my_basis = basis[held]
        my_eig = eig[held]
        my_scale = scale[held]
        own_draws[...] = draws[held, round_idx].astype(jnp.float32)
        old = own_effects[slot]
        prior = dot(old.astype(jnp.bfloat16), my_basis)
        coupled = dot_t((prior * my_eig).astype(jnp.bfloat16), my_basis)
        precision = my_eig + own_traits[0, my_rows, :][:, :1]
        jitter = own_draws[my_rows, :] / jnp.sqrt(precision)
        for step in range(1, people_n):
            part_copy(me, step, span_of(slot)).wait_recv()
        total = part[mine, :, :width]
        for step in range(1, people_n):
            total = total + gathered[step, :, :width]
        if slot == 0:
            squares = part[mine, :, width:]
            for step in range(1, people_n):
                squares = squares + gathered[step, :, width:]
            own_spread[...] = own_traits[1, my_rows, :] * jnp.sqrt(squares / people_total + 1e-06)
        spread = own_spread[...][:, :1]
        rotated = dot((my_scale * total + coupled).astype(jnp.bfloat16), my_basis)
        sampled = rotated / precision + spread * jitter
        fresh = dot_t(sampled.astype(jnp.bfloat16), my_basis)
        own_effects[slot] = fresh
        changes[bank, mine] = fresh - old
        for index in range(people_n):
            target = far_first(index, people_n)

            @pl.when(target != me)
            def _():
                change_copy(mine, target, bank).start()

    def change_of(slot, group):
        bank = slot % 2
        pieces = [changes[bank, group * subs + sub] for sub in range(subs)]
        return pieces[0] if subs == 1 else jnp.concatenate(pieces, axis=0)

    def take_changes(slot, group):
        bank = slot % 2
        block = group * WINDOW + slot
        for sub in range(subs):
            owner = group * subs + sub

            @pl.when(me != first + owner)
            def _():
                change_copy(owner, 0, bank).wait_recv()
                part_copy(first + owner, 1, span_of(slot)).wait_send()

        held = assignment[block]
        weighted = change_of(slot, group) * scale[held]
        shift = 2.0 * jnp.sum(weighted * freq[held], axis=1, keepdims=True)
        states[group] = (
            states[group] - dot_t(weighted.astype(jnp.bfloat16), genotype[held]) + shift
        )

    def settle(slot):
        for group in range(GROUPS_DEV):
            block = group * WINDOW + slot
            slot_effects[block] = slot_effects[block] + change_of(slot, group)

        @pl.when(owner_here)
        def _():
            for target in range(people_n):
                @pl.when(target != me)
                def _():
                    change_copy(mine, target, slot % 2).wait_send()

    for load in loads:
        load.wait()
    for block in range(blocks):
        slot_effects[block] = effects_in[assignment[block]]

    @pl.when(owner_here)
    def _():
        for slot in range(WINDOW):
            own_effects[slot] = slot_effects[my_group * WINDOW + slot, my_rows, :]

    pl.semaphore_wait(barrier, people_n - 1 + snps_n - 1)

    def round_body(round_idx, carry):
        squares = jnp.sum(residual[...] * residual[...], axis=1, keepdims=True)
        for slot in range(WINDOW):
            for group in range(GROUPS_DEV):
                if slot > 0:
                    take_changes(slot - 1, group)
                send_parts(slot, group, squares)
            if slot > 0:
                settle(slot - 1)

            @pl.when(owner_here)
            def _():
                sample(round_idx, slot)

        for group in range(GROUPS_DEV):
            take_changes(WINDOW - 1, group)
        bank = lax.rem(round_idx, 2)
        delta = states[0] - residual[...]
        for group in range(1, GROUPS_DEV):
            delta = delta + (states[group] - residual[...])
        deltas[bank, my_snps] = delta
        delta_copies = []
        for step in range(1, snps_n):
            copy = pltpu.make_async_remote_copy(
                src_ref=deltas.at[bank, my_snps],
                dst_ref=deltas.at[bank, my_snps],
                send_sem=delta_send.at[bank, step],
                recv_sem=delta_recv.at[bank, step],
                device_id={"snps": lax.rem(my_snps + step, snps_n)},
                device_id_type=MESH,
            )
            copy.start()
            delta_copies.append(copy)
        settle(WINDOW - 1)
        for copy in delta_copies:
            copy.wait()
        total = deltas[bank, 0]
        for index in range(1, snps_n):
            total = total + deltas[bank, index]
        fresh_residual = residual[...] + total
        residual[...] = fresh_residual
        for group in range(GROUPS_DEV):
            states[group] = fresh_residual
        return carry

    lax.fori_loop(0, rounds, round_body, 0)

    for target in range(blocks):
        effects[:, target * width:(target + 1) * width] = slot_effects[inverse[target]]


def owner_count(people_n, traits):
    return max(min(people_n // 2, GROUPS_DEV * traits // 8), GROUPS_DEV)


def per_device(people_n, snps_n, genotype, residual_init, effects_init, allele_freq, snp_scale,
               ld_basis, ld_eig, ridge, noise_scale, normal_draws, assignment):
    traits, people = residual_init.shape
    blocks, width = ld_basis.shape[0], ld_basis.shape[1]
    owners = owner_count(people_n, traits)
    rows = GROUPS_DEV * traits // owners
    slots = jnp.arange(blocks, dtype=jnp.int32)
    inverse = jnp.sum(
        jnp.where(assignment[None, :] == slots[:, None], slots[None, :], 0), axis=1, dtype=jnp.int32
    )
    by_block = lambda values: values.reshape(blocks, 1, width)
    row = lambda values: values.reshape(1, values.shape[0])
    vmem = pl.BlockSpec(memory_space=pltpu.MemorySpace.VMEM)
    smem = pl.BlockSpec(memory_space=pltpu.MemorySpace.SMEM)
    far = pl.BlockSpec(memory_space=pl.ANY)
    return pl.pallas_call(
        functools.partial(gibbs_kernel, people_n, snps_n, people * people_n),
        out_shape=[
            jax.ShapeDtypeStruct(effects_init.shape, jnp.float32),
            jax.ShapeDtypeStruct((traits, people), jnp.float32),
        ],
        in_specs=[far] * 4 + [vmem] * 6 + [smem] * 2,
        out_specs=[vmem] * 2,
        scratch_shapes=[
            pltpu.VMEM((blocks, people, width), genotype.dtype),
            pltpu.VMEM(ld_basis.shape, ld_basis.dtype),
            pltpu.VMEM((blocks,) + normal_draws.shape[:2] + (width,), normal_draws.dtype),
            pltpu.VMEM((blocks, traits, width), jnp.float32),
            pltpu.VMEM((blocks, 1, width), jnp.float32),
            pltpu.VMEM((blocks, traits, width), jnp.float32),
            pltpu.VMEM((GROUPS_DEV, traits, people), jnp.float32),
            pltpu.VMEM((owners, rows, width + 128), jnp.float32),
            pltpu.VMEM((people_n, rows, width + 128), jnp.float32),
            pltpu.VMEM((2, owners, rows, width), jnp.float32),
            pltpu.VMEM((2, snps_n, traits, people), jnp.float32),
            pltpu.VMEM((WINDOW, rows, width), jnp.float32),
            pltpu.VMEM((traits, width), jnp.float32),
            pltpu.VMEM((2, traits, 128), jnp.float32),
            pltpu.VMEM((rows, 128), jnp.float32),
            pltpu.SemaphoreType.DMA((3 * blocks + 1,)),
            pltpu.SemaphoreType.DMA((owners,)),
            pltpu.SemaphoreType.DMA((people_n,)),
            pltpu.SemaphoreType.DMA((2, people_n)),
            pltpu.SemaphoreType.DMA((2, owners)),
            pltpu.SemaphoreType.DMA((2, snps_n)),
            pltpu.SemaphoreType.DMA((2, snps_n)),
        ],
        compiler_params=pltpu.CompilerParams(
            collective_id=0, has_side_effects=True, vmem_limit_bytes=LIMIT
        ),
        name="gibbs",
    )(
        genotype, ld_basis, normal_draws, effects_init, by_block(allele_freq),
        by_block(snp_scale), by_block(ld_eig), row(ridge), row(noise_scale), residual_init,
        assignment, inverse,
    )


def solution(mesh):
    return jax.shard_map(
        functools.partial(per_device, mesh.shape["people"], mesh.shape["snps"]),
        mesh=mesh,
        in_specs=(
            P("people", "snps"),
            P(None, "people"),
            P(None, "snps"),
            P("snps"),
            P("snps"),
            P("snps", None, None),
            P("snps"),
            P(),
            P(),
            P(None, None, "snps"),
            P("snps"),
        ),
        out_specs=(P(None, "snps"), P(None, "people")),
        check_vma=False,
    )
```

```python
import functools

import jax
import jax.numpy as jnp
from jax import lax
from jax.experimental import pallas as pl
from jax.experimental.pallas import tpu as pltpu
from jax.sharding import PartitionSpec as P

WINDOW = 4
GROUPS_DEV = 2
LIMIT = 56 * 1024 * 1024
MESH = pl.DeviceIdType.MESH


def dot(left, right):
    return jnp.dot(left, right, preferred_element_type=jnp.float32)


def dot_t(left, right):
    return lax.dot_general(
        left, right, (((1,), (1,)), ((), ())), preferred_element_type=jnp.float32
    )


def as_column(row):
    size = row.shape[1]
    across = lax.broadcasted_iota(jnp.int32, (size, size), 1)
    down = lax.broadcasted_iota(jnp.int32, (size, size), 0)
    spread_out = jnp.broadcast_to(row, (size, size))
    return jnp.sum(jnp.where(across == down, spread_out, 0.0), axis=1, keepdims=True)


def gibbs_kernel(
    people_n, snps_n, people_total,
    genotype_hbm, basis_hbm, draws_hbm, effects_hbm, freq, snp_scale, eig, ridge, noise,
    residual_in, assignment, inverse,
    effects, residual,
    genotype, basis, draws, effects_in, scale, slot_effects, states, part, gathered, changes, deltas,
    own_effects, own_prior, own_draws, own_traits, own_spread,
    load_sem, part_send, part_recv, change_send, change_recv, delta_send, delta_recv,
):
    me = lax.axis_index("people")
    my_snps = lax.axis_index("snps")
    traits, people = residual_in.shape
    blocks, width = basis.shape[0], basis.shape[1]
    rounds = draws.shape[1]
    owners, rows = part.shape[0], part.shape[1]
    first = (people_n - owners) // 2
    subs = owners // GROUPS_DEV
    owner_here = (me >= first) & (me < first + owners)
    mine = me - first
    my_group = mine // subs
    my_rows = pl.ds((mine % subs) * rows, rows)

    loads = [pltpu.make_async_copy(basis_hbm, basis, load_sem.at[3 * blocks])]
    for block in range(blocks):
        cols = pl.ds(block * width, width)
        loads += [
            pltpu.make_async_copy(effects_hbm.at[:, cols], effects_in.at[block], load_sem.at[block]),
            pltpu.make_async_copy(
                genotype_hbm.at[:, cols], genotype.at[block], load_sem.at[blocks + block]
            ),
            pltpu.make_async_copy(
                draws_hbm.at[:, :, cols], draws.at[block], load_sem.at[2 * blocks + block]
            ),
        ]
    for load in loads:
        load.start()

    barrier = pltpu.get_barrier_semaphore()
    for step in range(1, people_n):
        pl.semaphore_signal(
            barrier, inc=1, device_id={"people": lax.rem(me + step, people_n)},
            device_id_type=MESH,
        )
    for step in range(1, snps_n):
        pl.semaphore_signal(
            barrier, inc=1, device_id={"snps": lax.rem(my_snps + step, snps_n)},
            device_id_type=MESH,
        )

    allele = freq[...]
    scale[...] = snp_scale[...] / jnp.sqrt(people_total * 2.0 * allele * (1.0 - allele))
    residual[...] = residual_in[...]
    for group in range(GROUPS_DEV):
        states[group] = residual_in[...]
    own_traits[0] = jnp.broadcast_to(as_column(ridge[...]), (traits, 128))
    own_traits[1] = jnp.broadcast_to(as_column(noise[...]), (traits, 128))

    def part_copy(owner, step, span):
        return pltpu.make_async_remote_copy(
            src_ref=part.at[owner - first, :, pl.ds(0, span)],
            dst_ref=gathered.at[step, :, pl.ds(0, span)],
            send_sem=part_send.at[owner - first],
            recv_sem=part_recv.at[step],
            device_id={"people": owner},
            device_id_type=MESH,
        )

    def change_copy(owner, target, bank):
        return pltpu.make_async_remote_copy(
            src_ref=changes.at[bank, owner],
            dst_ref=changes.at[bank, owner],
            send_sem=change_send.at[bank, target],
            recv_sem=change_recv.at[bank, owner],
            device_id={"people": target},
            device_id_type=MESH,
        )

    def far_first(index, count):
        return jnp.where(me < people_n // 2, count - 1 - index, index)

    def span_of(slot):
        return width + 128 if slot == 0 else width

    def send_parts(slot, group, squares):
        block = group * WINDOW + slot
        held = assignment[block]
        state = states[group]
        cross = dot(state.astype(jnp.bfloat16), genotype[held])
        cross = cross - 2.0 * freq[held] * jnp.sum(state, axis=1, keepdims=True)
        for sub in range(subs):
            owner = group * subs + sub
            part[owner, :, :width] = cross[sub * rows:(sub + 1) * rows]
            if slot == 0:
                part[owner, :, width:] = jnp.broadcast_to(
                    squares[sub * rows:(sub + 1) * rows], (rows, 128)
                )
        for index in range(subs):
            owner = first + group * subs + far_first(index, subs)

            @pl.when(owner != me)
            def _():
                part_copy(owner, lax.rem(me - owner + people_n, people_n), span_of(slot)).start()

    def prepare(round_idx, slot):
        held = assignment[my_group * WINDOW + slot]
        my_basis = basis[held]
        my_eig = eig[held]
        own_draws[...] = draws[held, round_idx].astype(jnp.float32)
        prior = dot(own_effects[slot].astype(jnp.bfloat16), my_basis)
        own_prior[0] = dot_t((prior * my_eig).astype(jnp.bfloat16), my_basis)
        precision = my_eig + own_traits[0, my_rows, :][:, :1]
        own_prior[1] = precision
        own_prior[2] = own_draws[my_rows, :] / jnp.sqrt(precision)

    def sample(slot):
        bank = slot % 2
        held = assignment[my_group * WINDOW + slot]
        my_basis = basis[held]
        my_scale = scale[held]
        old = own_effects[slot]
        for step in range(1, people_n):
            part_copy(me, step, span_of(slot)).wait_recv()
        total = part[mine, :, :width]
        for step in range(1, people_n):
            total = total + gathered[step, :, :width]
        if slot == 0:
            squares = part[mine, :, width:]
            for step in range(1, people_n):
                squares = squares + gathered[step, :, width:]
            own_spread[...] = own_traits[1, my_rows, :] * jnp.sqrt(squares / people_total + 1e-06)
        spread = own_spread[...][:, :1]
        rotated = dot((my_scale * total + own_prior[0]).astype(jnp.bfloat16), my_basis)
        sampled = rotated / own_prior[1] + spread * own_prior[2]
        fresh = dot_t(sampled.astype(jnp.bfloat16), my_basis)
        own_effects[slot] = fresh
        changes[bank, mine] = fresh - old
        for index in range(people_n):
            target = far_first(index, people_n)

            @pl.when(target != me)
            def _():
                change_copy(mine, target, bank).start()

    def change_of(slot, group):
        bank = slot % 2
        pieces = [changes[bank, group * subs + sub] for sub in range(subs)]
        return pieces[0] if subs == 1 else jnp.concatenate(pieces, axis=0)

    def take_changes(slot, group):
        bank = slot % 2
        block = group * WINDOW + slot
        for sub in range(subs):
            owner = group * subs + sub

            @pl.when(me != first + owner)
            def _():
                change_copy(owner, 0, bank).wait_recv()
                part_copy(first + owner, 1, span_of(slot)).wait_send()

        held = assignment[block]
        weighted = change_of(slot, group) * scale[held]
        shift = 2.0 * jnp.sum(weighted * freq[held], axis=1, keepdims=True)
        states[group] = (
            states[group] - dot_t(weighted.astype(jnp.bfloat16), genotype[held]) + shift
        )

    def settle(slot):
        for group in range(GROUPS_DEV):
            block = group * WINDOW + slot
            slot_effects[block] = slot_effects[block] + change_of(slot, group)

        @pl.when(owner_here)
        def _():
            for target in range(people_n):
                @pl.when(target != me)
                def _():
                    change_copy(mine, target, slot % 2).wait_send()

    for load in loads:
        load.wait()
    for block in range(blocks):
        slot_effects[block] = effects_in[assignment[block]]

    @pl.when(owner_here)
    def _():
        for slot in range(WINDOW):
            own_effects[slot] = slot_effects[my_group * WINDOW + slot, my_rows, :]
        prepare(0, 0)

    pl.semaphore_wait(barrier, people_n - 1 + snps_n - 1)

    def round_body(round_idx, carry):
        squares = jnp.sum(residual[...] * residual[...], axis=1, keepdims=True)
        for slot in range(WINDOW):
            for group in range(GROUPS_DEV):
                if slot > 0:
                    take_changes(slot - 1, group)
                send_parts(slot, group, squares)

            @pl.when(owner_here)
            def _():
                sample(slot)
                if slot < WINDOW - 1:
                    prepare(round_idx, slot + 1)

            if slot > 0:
                settle(slot - 1)

        for group in range(GROUPS_DEV):
            take_changes(WINDOW - 1, group)
        bank = lax.rem(round_idx, 2)
        delta = states[0] - residual[...]
        for group in range(1, GROUPS_DEV):
            delta = delta + (states[group] - residual[...])
        deltas[bank, my_snps] = delta
        delta_copies = []
        for step in range(1, snps_n):
            copy = pltpu.make_async_remote_copy(
                src_ref=deltas.at[bank, my_snps],
                dst_ref=deltas.at[bank, my_snps],
                send_sem=delta_send.at[bank, step],
                recv_sem=delta_recv.at[bank, step],
                device_id={"snps": lax.rem(my_snps + step, snps_n)},
                device_id_type=MESH,
            )
            copy.start()
            delta_copies.append(copy)
        settle(WINDOW - 1)

        @pl.when(owner_here)
        def _():
            prepare(lax.rem(round_idx + 1, rounds), 0)

        for copy in delta_copies:
            copy.wait()
        total = deltas[bank, 0]
        for index in range(1, snps_n):
            total = total + deltas[bank, index]
        fresh_residual = residual[...] + total
        residual[...] = fresh_residual
        for group in range(GROUPS_DEV):
            states[group] = fresh_residual
        return carry

    lax.fori_loop(0, rounds, round_body, 0)

    for target in range(blocks):
        effects[:, target * width:(target + 1) * width] = slot_effects[inverse[target]]


def owner_count(people_n, traits):
    return max(min(people_n // 2, GROUPS_DEV * traits // 8), GROUPS_DEV)


def per_device(people_n, snps_n, genotype, residual_init, effects_init, allele_freq, snp_scale,
               ld_basis, ld_eig, ridge, noise_scale, normal_draws, assignment):
    traits, people = residual_init.shape
    blocks, width = ld_basis.shape[0], ld_basis.shape[1]
    owners = owner_count(people_n, traits)
    rows = GROUPS_DEV * traits // owners
    slots = jnp.arange(blocks, dtype=jnp.int32)
    inverse = jnp.sum(
        jnp.where(assignment[None, :] == slots[:, None], slots[None, :], 0), axis=1, dtype=jnp.int32
    )
    by_block = lambda values: values.reshape(blocks, 1, width)
    row = lambda values: values.reshape(1, values.shape[0])
    vmem = pl.BlockSpec(memory_space=pltpu.MemorySpace.VMEM)
    smem = pl.BlockSpec(memory_space=pltpu.MemorySpace.SMEM)
    far = pl.BlockSpec(memory_space=pl.ANY)
    return pl.pallas_call(
        functools.partial(gibbs_kernel, people_n, snps_n, people * people_n),
        out_shape=[
            jax.ShapeDtypeStruct(effects_init.shape, jnp.float32),
            jax.ShapeDtypeStruct((traits, people), jnp.float32),
        ],
        in_specs=[far] * 4 + [vmem] * 6 + [smem] * 2,
        out_specs=[vmem] * 2,
        scratch_shapes=[
            pltpu.VMEM((blocks, people, width), genotype.dtype),
            pltpu.VMEM(ld_basis.shape, ld_basis.dtype),
            pltpu.VMEM((blocks,) + normal_draws.shape[:2] + (width,), normal_draws.dtype),
            pltpu.VMEM((blocks, traits, width), jnp.float32),
            pltpu.VMEM((blocks, 1, width), jnp.float32),
            pltpu.VMEM((blocks, traits, width), jnp.float32),
            pltpu.VMEM((GROUPS_DEV, traits, people), jnp.float32),
            pltpu.VMEM((owners, rows, width + 128), jnp.float32),
            pltpu.VMEM((people_n, rows, width + 128), jnp.float32),
            pltpu.VMEM((2, owners, rows, width), jnp.float32),
            pltpu.VMEM((2, snps_n, traits, people), jnp.float32),
            pltpu.VMEM((WINDOW, rows, width), jnp.float32),
            pltpu.VMEM((3, rows, width), jnp.float32),
            pltpu.VMEM((traits, width), jnp.float32),
            pltpu.VMEM((2, traits, 128), jnp.float32),
            pltpu.VMEM((rows, 128), jnp.float32),
            pltpu.SemaphoreType.DMA((3 * blocks + 1,)),
            pltpu.SemaphoreType.DMA((owners,)),
            pltpu.SemaphoreType.DMA((people_n,)),
            pltpu.SemaphoreType.DMA((2, people_n)),
            pltpu.SemaphoreType.DMA((2, owners)),
            pltpu.SemaphoreType.DMA((2, snps_n)),
            pltpu.SemaphoreType.DMA((2, snps_n)),
        ],
        compiler_params=pltpu.CompilerParams(
            collective_id=0, has_side_effects=True, vmem_limit_bytes=LIMIT
        ),
        name="gibbs",
    )(
        genotype, ld_basis, normal_draws, effects_init, by_block(allele_freq),
        by_block(snp_scale), by_block(ld_eig), row(ridge), row(noise_scale), residual_init,
        assignment, inverse,
    )


def solution(mesh):
    return jax.shard_map(
        functools.partial(per_device, mesh.shape["people"], mesh.shape["snps"]),
        mesh=mesh,
        in_specs=(
            P("people", "snps"),
            P(None, "people"),
            P(None, "snps"),
            P("snps"),
            P("snps"),
            P("snps", None, None),
            P("snps"),
            P(),
            P(),
            P(None, None, "snps"),
            P("snps"),
        ),
        out_specs=(P(None, "snps"), P(None, "people")),
        check_vma=False,
    )
```
